256 devices in a mesh: dom: 64 (over z, x, core), grp: 4 (over y).
Axes of the slice: x: 4, y: 4, z: 8, core: 2. Of those that a mesh axis runs over, the one named last changes fastest.
Arguments:
- blocks: bfloat16 [12288, 6, 128, 128], P(('dom', 'grp')), may hold values from -0.21875 to 0.21875
- local_cols: int32 [12288, 4], P(('dom', 'grp')), may hold values from 0 to 191
- remote_refs: int32 [12288, 2], P(('dom', 'grp')), may hold values from 0 to 191
- send_blocks: int32 [64, 4, 64, 3], P('dom', 'grp'), may hold values from 0 to 47
- send_counts: int32 [64, 4, 64], P('dom', 'grp'), may hold values from 0 to 3
- probes: bfloat16 [64, 1572864], P(None, ('dom', 'grp')), may hold values from -6 to 6
Outputs:
- moments: float32 [3, 1572864], P(None, ('dom', 'grp'))
The draws below stay inside these ranges and needn't reach their ends.
All inputs are finite; a program needn't handle non-finite values.
Results may differ from the reference program's by a relative error of at most 0.00064.
Values may be sent and summed in bfloat16 or wider, within the bound.
No kernel may reach another device: no remote copies, remote signals or barrier semaphores. Data moves between devices by JAX's collectives and lax.ppermute only.
A program may use at most 64 MiB of HBM per device.

```python
import math
import jax
import jax.numpy as jnp
from jax import lax

BS = 128
PROBES = 64
BR_DEV = 48
LOCAL = 4
REMOTE = 2
CAP = 3
KMOM = 256
PARTS_SIZE = 64
LANES = 4
BR_PART = 192
NB = 12288
NODES = 1572864
SLOTS = 192
NNZ = 6


def touch_ends(entries, key, least, high):
    longest = entries.shape.index(max(entries.shape))
    spots = []
    for shift in (0, 1):
        where = [jax.random.randint(jax.random.fold_in(key, axis), (), 0, length) for axis, length in enumerate(entries.shape)]
        where[longest] = (where[longest] + shift) % entries.shape[longest]
        spots.append(tuple(where))
    return entries.at[spots[0]].set(least).at[spots[1]].set(high)


def steps_of(key, extent, shards, least, top_value):
    loudness = 1.0
    for axis_at, blocks in shards:
        draws = jax.random.uniform(jax.random.fold_in(jax.random.fold_in(key, 6), axis_at), (blocks,), jnp.float32, least / len(shards), top_value / len(shards))
        loudness = loudness * jnp.repeat(jnp.exp(draws), extent[axis_at] // blocks).reshape((-1,) + (1,) * (len(extent) - 1 - axis_at))
    return loudness


def noise(own_key, extent, deviation, most, shards=(), kind=jnp.bfloat16):
    drawn = jax.random.normal(own_key, extent, jnp.float32) * deviation
    if len(shards) > 0:
        drawn = steps_of(own_key, extent, shards, -0.22, 0.18) * drawn
    return jnp.clip(drawn, min=-most, max=most).astype(kind)


def setup_inputs(seed: int = 0) -> dict:
    seeds = jax.random.split(jax.random.key(seed), 7)
    return {
        "blocks": noise(seeds[0], (NB, NNZ, BS, BS), (NNZ * BS) ** -0.5, 0.21875, ((0, 256),)),
        "local_cols": touch_ends(jax.random.randint(seeds[1], (NB, LOCAL), 0, BR_PART), jax.random.fold_in(seeds[1], 1), 0, BR_PART - 1).astype(jnp.int32),
        "remote_refs": touch_ends(jax.random.randint(seeds[2], (NB, REMOTE), 0, SLOTS), jax.random.fold_in(seeds[2], 1), 0, SLOTS - 1).astype(jnp.int32),
        "send_blocks": touch_ends(jax.random.randint(seeds[3], (PARTS_SIZE, LANES, PARTS_SIZE, CAP), 0, BR_DEV), jax.random.fold_in(seeds[3], 1), 0, BR_DEV - 1).astype(jnp.int32),
        "send_counts": touch_ends(jax.random.randint(seeds[4], (PARTS_SIZE, LANES, PARTS_SIZE), 0, CAP + 1), jax.random.fold_in(seeds[4], 1), 0, CAP).astype(jnp.int32),
        "probes": noise(seeds[5], (PROBES, NODES), 1.0, 6.0, ((1, 256),)),
    }


def jackson(order, total):
    angle = math.pi / (total + 1)
    return ((total - order + 1) * math.cos(order * angle) + math.sin(order * angle) / math.tan(angle)) / (total + 1)

def reference(blocks, local_cols, remote_refs, send_blocks, send_counts, probes):
    rows = jnp.arange(NB, dtype=jnp.int32)
    part = rows // BR_PART
    lane = rows // BR_DEV % LANES
    local_global = part[:, None] * BR_PART + local_cols
    peer = remote_refs // CAP
    slot = remote_refs % CAP
    source = send_blocks[peer, lane[:, None], part[:, None], slot]
    remote_global = peer * BR_PART + lane[:, None] * BR_DEV + source
    live = (slot < send_counts[peer, lane[:, None], part[:, None]]).astype(jnp.float32)
    columns = jnp.concatenate([local_global.astype(jnp.int32), remote_global.astype(jnp.int32)], axis=1).astype(jnp.int32)
    weights = jnp.concatenate([jnp.ones((NB, LOCAL), jnp.float32), live], axis=1).astype(jnp.float32)
    groups = PARTS_SIZE * LANES
    grouped_blocks = blocks.reshape(groups, BR_DEV, NNZ, BS, BS)
    grouped_cols = columns.reshape(groups, BR_DEV, NNZ)
    grouped_weights = weights.reshape(groups, BR_DEV, NNZ)

    def apply_op(field):
        field_blocks = field.reshape(PROBES, NB, BS)

        def one_group(items):
            block_set, col_set, weight_set = items
            picked = jnp.take(field_blocks, col_set, axis=1).astype(jnp.float32)
            picked = picked * weight_set[None, :, :, None]
            return jnp.einsum('rjab,prjb->pra', block_set.astype(jnp.float32), picked)
        result = lax.map(one_group, (grouped_blocks, grouped_cols, grouped_weights))
        return jnp.transpose(result, (1, 0, 2, 3)).reshape(PROBES, NODES)
    first = apply_op(probes).astype(jnp.bfloat16)
    second = 2.0 * apply_op(first) - probes.astype(jnp.float32)
    base = probes.astype(jnp.float32)
    norm = 1.0 / math.sqrt(PROBES)
    moment_zero = jackson(0, KMOM) * norm * lax.optimization_barrier(jnp.sum(base * base, axis=0))
    moment_one = 2.0 * jackson(1, KMOM) * norm * lax.optimization_barrier(jnp.sum(base * first.astype(jnp.float32), axis=0))
    moment_two = 2.0 * jackson(2, KMOM) * norm * lax.optimization_barrier(jnp.sum(base * second, axis=0))
    return jnp.stack([moment_zero, moment_one, moment_two], axis=0)
```

```python
import functools
import math

import jax
import jax.numpy as jnp
from jax import lax
from jax.experimental import pallas as pl
from jax.experimental.pallas import tpu as pltpu
from jax.sharding import PartitionSpec as P

PROBES = 64
LOCAL = 4
REMOTE = 2
KMOM = 256
LANES = 4
STEP = 8


def grant(mib):
    return pltpu.CompilerParams(vmem_limit_bytes=mib * 1024 * 1024)


HBM = pl.BlockSpec(memory_space=pltpu.HBM)
VMEM = pl.BlockSpec(memory_space=pltpu.VMEM)
SMEM = pl.BlockSpec(memory_space=pltpu.SMEM)
DMA = pltpu.SemaphoreType.DMA


def jackson(order, total):
    angle = math.pi / (total + 1)
    return (
        (total - order + 1) * math.cos(order * angle) + math.sin(order * angle) / math.tan(angle)
    ) / (total + 1)


def pair_dot(fields, mats):
    left = jnp.concatenate(fields, axis=1)
    right = jnp.concatenate(mats, axis=1)
    return lax.dot_general(left, right, (((1,), (1,)), ((), ())), preferred_element_type=jnp.float32)


def start_sends(table_ref, count_ref, src_ref, send_ref, sem):
    rows = src_ref.shape[0] - 1
    peers, slots = send_ref.shape[0], send_ref.shape[1]

    @pl.loop(0, peers, unroll=4)
    def _(d):
        count = count_ref[d]
        for s in range(slots):
            index = jnp.where(s < count, table_ref[s, 0, d], rows)
            pltpu.make_async_copy(src_ref.at[index], send_ref.at[d, s], sem).start()


def wait_sends(send_ref, sem):
    pltpu.make_async_copy(send_ref, send_ref, sem).wait()


def pack_kernel(table_ref, count_ref, probes_ref, own_ref, send_ref, src_ref, own_sem, send_sem):
    rows, _, size = own_ref.shape
    for r in range(rows):
        src_ref[r] = probes_ref[:, r * size:(r + 1) * size]
    src_ref[rows] = jnp.zeros_like(src_ref[rows])
    start_sends(table_ref, count_ref, src_ref, send_ref, send_sem)
    own = pltpu.make_async_copy(src_ref.at[pl.ds(0, rows)], own_ref, own_sem)
    own.start()
    own.wait()
    wait_sends(send_ref, send_sem)


def pack(table, counts, probes, peers, slots, rows, size):
    part = probes.shape[0]
    return pl.pallas_call(
        pack_kernel,
        in_specs=[SMEM, SMEM, VMEM],
        out_specs=[HBM, HBM],
        scratch_shapes=[pltpu.VMEM((rows + 1, part, size), probes.dtype), DMA, DMA],
        out_shape=[pltpu.HBM((rows, part, size), probes.dtype), pltpu.HBM((peers, slots, part, size), probes.dtype)],
        compiler_params=grant(62),
        name="pack",
    )(table, counts, probes)


def block_copy(blocks_ref, held_ref, sem, first, count, step):
    rows = pl.ds(step * STEP, STEP)
    return pltpu.make_async_copy(blocks_ref.at[rows, pl.ds(first, count)], held_ref.at[rows], sem.at[step])


def local_products(lane_ref, pieces, blocks_ref, panel_ref, held_ref, panel_sem, sem, cols_ref, use):
    rows = pieces[0].shape[0]
    steps = rows // STEP
    me = lane_ref[0]
    copies = []
    for shift, piece in enumerate(pieces):
        lane = lax.rem(me + LANES - shift, LANES)
        copies.append(pltpu.make_async_copy(piece, panel_ref.at[pl.ds(lane * rows, rows)], panel_sem.at[shift]))
    for copy in copies:
        copy.start()
    for step in range(steps):
        block_copy(blocks_ref, held_ref, sem, 0, LOCAL, step).start()
    for copy in copies:
        copy.wait()

    @pl.loop(0, steps)
    def _(step):
        block_copy(blocks_ref, held_ref, sem, 0, LOCAL, step).wait()
        for t in range(STEP):
            r = step * STEP + t
            total = None
            for j in range(0, LOCAL, 2):
                term = pair_dot(
                    [panel_ref[cols_ref[j + k, r]] for k in range(2)],
                    [held_ref[r, j + k] for k in range(2)],
                )
                total = term if total is None else total + term
            use(r, total)


def local_kernel(cols_ref, lane_ref, own_ref, prev_ref, across_ref, next_ref, blocks_ref, sum_ref, panel_ref, held_ref, panel_sem, sem):
    def use(r, total):
        sum_ref[r] = total

    local_products(
        lane_ref, (own_ref, prev_ref, across_ref, next_ref), blocks_ref, panel_ref, held_ref, panel_sem, sem, cols_ref, use
    )


def local_scratch(rows, part, size, kind):
    return [
        pltpu.VMEM((LANES * rows, part, size), kind),
        pltpu.VMEM((rows, LOCAL, size, size), kind),
        DMA((LANES,)),
        DMA((rows // STEP,)),
    ]


def in_hbm(x):
    return pltpu.with_memory_space_constraint(x, pltpu.HBM)


def in_vmem(x):
    return pltpu.with_memory_space_constraint(x, pltpu.VMEM)


def local_part(cols, lane, pieces, blocks):
    rows, part, size = pieces[0].shape
    return pl.pallas_call(
        local_kernel,
        in_specs=[SMEM, SMEM] + [HBM] * 5,
        out_specs=VMEM,
        scratch_shapes=local_scratch(rows, part, size, blocks.dtype),
        out_shape=jax.ShapeDtypeStruct((rows, part, size), jnp.float32),
        compiler_params=grant(24),
        name="local",
    )(cols, lane, *[in_hbm(x) for x in pieces], in_hbm(blocks))


def remote_products(refs_ref, got_ref, blocks_ref, other_ref, far_ref, near_ref, far_sem, near_sem, use):
    rows = near_ref.shape[0]
    steps = rows // STEP

    def near_copy(step):
        at = pl.ds(step * STEP, STEP)
        return pltpu.make_async_copy(other_ref.at[at], near_ref.at[at], near_sem.at[step])

    for step in range(steps):
        block_copy(blocks_ref, far_ref, far_sem, LOCAL, REMOTE, step).start()
        near_copy(step).start()

    @pl.loop(0, steps)
    def _(step):
        block_copy(blocks_ref, far_ref, far_sem, LOCAL, REMOTE, step).wait()
        near_copy(step).wait()
        for t in range(STEP):
            r = step * STEP + t
            total = pair_dot(
                [got_ref[refs_ref[j, r]] for j in range(REMOTE)],
                [far_ref[r, j] for j in range(REMOTE)],
            )
            use(r, total, near_ref[r])


def remote_scratch(rows, part, size, kind, near_kind):
    return [
        pltpu.VMEM((rows, REMOTE, size, size), kind),
        pltpu.VMEM((rows, part, size), near_kind),
        DMA((rows // STEP,)),
        DMA((rows // STEP,)),
    ]


def first_kernel(refs_ref, table_ref, count_ref, got_ref, sum_ref, blocks_ref, own_ref, send_ref, src_ref, own_sem, send_sem, *scratch):
    rows = own_ref.shape[0]
    src_ref[rows] = jnp.zeros_like(src_ref[rows])

    def use(r, total, near):
        src_ref[r] = (near + total).astype(src_ref.dtype)

    remote_products(refs_ref, got_ref, blocks_ref, sum_ref, *scratch, use)
    start_sends(table_ref, count_ref, src_ref, send_ref, send_sem)
    own = pltpu.make_async_copy(src_ref.at[pl.ds(0, rows)], own_ref, own_sem)
    own.start()
    own.wait()
    wait_sends(send_ref, send_sem)


def first_part(refs, table, counts, got, sums, blocks, peers, slots):
    rows, part, size = sums.shape
    return pl.pallas_call(
        first_kernel,
        in_specs=[SMEM, SMEM, SMEM, VMEM, HBM, HBM],
        out_specs=[HBM, HBM],
        scratch_shapes=[pltpu.VMEM((rows + 1, part, size), got.dtype), DMA, DMA]
        + remote_scratch(rows, part, size, blocks.dtype, sums.dtype),
        out_shape=[pltpu.HBM((rows, part, size), got.dtype), pltpu.HBM((peers, slots, part, size), got.dtype)],
        compiler_params=grant(24),
        name="first",
    )(refs, table, counts, in_vmem(got), in_hbm(sums), in_hbm(blocks))


def near_kernel(cols_ref, lane_ref, own_ref, prev_ref, across_ref, next_ref, blocks_ref, probes_ref, near_ref, base_ref, panel_ref, held_ref, base_sem, panel_sem, sem):
    rows, _, size = base_ref.shape
    copy = pltpu.make_async_copy(probes_ref, base_ref, base_sem)
    copy.start()
    copy.wait()
    me = lane_ref[0]

    def use(r, total):
        base = base_ref[r].astype(jnp.float32)
        one = panel_ref[me * rows + r].astype(jnp.float32)
        at = pl.ds(pl.multiple_of(r * size, size), size)
        for k, other in enumerate((base, one, 2.0 * total - base)):
            near_ref[k:k + 1, at] = jnp.sum(base * other, axis=0, keepdims=True)

    local_products(
        lane_ref, (own_ref, prev_ref, across_ref, next_ref), blocks_ref, panel_ref, held_ref, panel_sem, sem, cols_ref, use
    )


def near_part(cols, lane, pieces, blocks, base):
    rows, part, size = pieces[0].shape
    panel, held, panel_sem, sem = local_scratch(rows, part, size, blocks.dtype)
    return pl.pallas_call(
        near_kernel,
        in_specs=[SMEM, SMEM] + [HBM] * 6,
        out_specs=VMEM,
        scratch_shapes=[pltpu.VMEM(base.shape, base.dtype), panel, held, DMA, panel_sem, sem],
        out_shape=jax.ShapeDtypeStruct((3, rows * size), jnp.float32),
        compiler_params=grant(24),
        name="near",
    )(cols, lane, *[in_hbm(x) for x in pieces], in_hbm(blocks), in_hbm(base))


def moments_kernel(scale, refs_ref, got_ref, near_ref, base_ref, blocks_ref, out_ref, *scratch):
    out_ref[0:1] = near_ref[0:1] * scale[0]
    out_ref[1:2] = near_ref[1:2] * scale[1]
    size = base_ref.shape[2]

    def use(r, total, base):
        at = pl.ds(pl.multiple_of(r * size, size), size)
        value = near_ref[2:3, at] + 2.0 * jnp.sum(total * base.astype(jnp.float32), axis=0, keepdims=True)
        out_ref[2:3, at] = value * scale[2]

    remote_products(refs_ref, got_ref, blocks_ref, base_ref, *scratch, use)


def moments_part(refs, got, near, base, blocks, scale):
    rows, part, size = base.shape
    return pl.pallas_call(
        functools.partial(moments_kernel, scale),
        in_specs=[SMEM, VMEM, VMEM, HBM, HBM],
        out_specs=VMEM,
        scratch_shapes=remote_scratch(rows, part, size, blocks.dtype, base.dtype),
        out_shape=jax.ShapeDtypeStruct(near.shape, near.dtype),
        compiler_params=grant(24),
        name="moments",
    )(refs, in_vmem(got), near, in_hbm(base), in_hbm(blocks))


def on_device(blocks, local_cols, remote_refs, send_blocks, send_counts, probes):
    rows, _, size, _ = blocks.shape
    peers, slots = send_blocks.shape[2], send_blocks.shape[3]
    table = send_blocks.transpose(0, 3, 1, 2)[0]
    counts = send_counts[0, 0]
    cols = local_cols.T
    refs = remote_refs.T
    lane = lax.axis_index("grp").astype(jnp.int32).reshape(1)
    norm = 1.0 / math.sqrt(PROBES)
    scale = (
        jackson(0, KMOM) * norm,
        2.0 * jackson(1, KMOM) * norm,
        2.0 * jackson(2, KMOM) * norm,
    )

    def exchange(send):
        got = lax.all_to_all(send, "dom", split_axis=0, concat_axis=0, tiled=True)
        return got.reshape(peers * slots, send.shape[2], size)

    def panel(own):
        pieces = [own]
        for shift in (1, 2, 3):
            pieces.append(lax.ppermute(own, "grp", [(i, (i + shift) % LANES) for i in range(LANES)]))
        return pieces

    base, send = pack(table, counts, probes, peers, slots, rows, size)
    got = exchange(send)
    sums = local_part(cols, lane, panel(base), blocks)
    first, send = first_part(refs, table, counts, got, sums, blocks, peers, slots)
    got = exchange(send)
    near = near_part(cols, lane, panel(first), blocks, base)
    return moments_part(refs, got, near, base, blocks, scale)


def solution(mesh):
    in_specs = (
        P(("dom", "grp"), None, None, None),
        P(("dom", "grp"), None),
        P(("dom", "grp"), None),
        P("dom", "grp", None, None),
        P("dom", "grp", None),
        P(None, ("dom", "grp")),
    )
    out_specs = P(None, ("dom", "grp"))
    return jax.shard_map(
        on_device, mesh=mesh, in_specs=in_specs, out_specs=out_specs, check_vma=False
    )
```

```python
import functools
import math

import jax
import jax.numpy as jnp
from jax import lax
from jax.experimental import pallas as pl
from jax.experimental.pallas import tpu as pltpu
from jax.sharding import PartitionSpec as P


PROBES = 64
LOCAL = 4
REMOTE = 2
KMOM = 256
LANES = 4
STEP = 8
WIDE = 48
ZS, XS, CS = 8, 4, 2
PLANE = XS * CS
EARLY, LATE = (1, 7, 2, 6), (3, 5, 4)


def grant(mib):
    return pltpu.CompilerParams(vmem_limit_bytes=mib * 1024 * 1024)


HBM = pl.BlockSpec(memory_space=pltpu.HBM)
VMEM = pl.BlockSpec(memory_space=pltpu.VMEM)
SMEM = pl.BlockSpec(memory_space=pltpu.SMEM)
DMA = pltpu.SemaphoreType.DMA


def jackson(order, total):
    angle = math.pi / (total + 1)
    return (
        (total - order + 1) * math.cos(order * angle) + math.sin(order * angle) / math.tan(angle)
    ) / (total + 1)


def pair_dot(fields, mats):
    left = jnp.concatenate(fields, axis=1)
    right = jnp.concatenate(mats, axis=1)
    return lax.dot_general(left, right, (((1,), (1,)), ((), ())), preferred_element_type=jnp.float32)


def slot_block(table_ref, count_ref, d, s, rows):
    return jnp.where(s < count_ref[d], table_ref[s, 0, d], rows)


def start_wide(table_ref, count_ref, src_ref, send_ref, sem):
    rows = src_ref.shape[0] - 1
    peers, slots, part, _ = send_ref.shape
    probes = pl.ds(0, part)

    @pl.loop(0, peers, unroll=4)
    def _(d):
        for s in range(slots):
            index = slot_block(table_ref, count_ref, d, s, rows)
            pltpu.make_async_copy(src_ref.at[index, probes], send_ref.at[d, s], sem).start()


def start_slim(first, table_ref, count_ref, me_ref, src_ref, turn_refs, sem):
    rows = src_ref.shape[0] - 1
    part = turn_refs[0].shape[1]
    slots = turn_refs[0].shape[0] // ZS
    me = me_ref[0]
    probes = pl.ds(first, part)

    @pl.loop(0, ZS)
    def _(dz):
        z = (me // PLANE + dz) & (ZS - 1)
        for k, ref in enumerate(turn_refs):
            x = (me // CS + k // CS) & (XS - 1)
            core = (me + k) & (CS - 1)
            d = z * PLANE + x * CS + core
            for s in range(slots):
                index = slot_block(table_ref, count_ref, d, s, rows)
                pltpu.make_async_copy(src_ref.at[index, probes], ref.at[dz * slots + s], sem).start()


def wait_all(refs, sem):
    for ref in refs:
        pltpu.make_async_copy(ref, ref, sem).wait()


def load_fields(probes_ref, src_ref):
    rows, size = src_ref.shape[0] - 1, src_ref.shape[2]
    for r in range(rows):
        src_ref[r] = probes_ref[:, r * size:(r + 1) * size]
    src_ref[rows] = jnp.zeros_like(src_ref[rows])


def pack_wide_kernel(table_ref, count_ref, probes_ref, send_ref, src_ref, send_sem):
    load_fields(probes_ref, src_ref)
    start_wide(table_ref, count_ref, src_ref, send_ref, send_sem)
    wait_all([send_ref], send_sem)


def pack_wide(table, counts, probes, peers, slots, rows, size):
    kind = probes.dtype
    return pl.pallas_call(
        pack_wide_kernel,
        grid=(1,),
        in_specs=[SMEM, SMEM, pl.BlockSpec((WIDE, probes.shape[1]), lambda i: (0, 0))],
        out_specs=HBM,
        scratch_shapes=[pltpu.VMEM((rows + 1, WIDE, size), kind), DMA],
        out_shape=pltpu.HBM((peers, slots, WIDE, size), kind),
        compiler_params=grant(62),
        name="pack_wide",
    )(table, counts, probes)


def pack_slim_kernel(table_ref, count_ref, me_ref, probes_ref, own_ref, *rest):
    turn_refs, (src_ref, own_sem, turn_sem) = rest[:PLANE], rest[PLANE:]
    rows = own_ref.shape[0]
    load_fields(probes_ref, src_ref)
    own = pltpu.make_async_copy(src_ref.at[pl.ds(0, rows)], own_ref, own_sem)
    own.start()
    start_slim(WIDE, table_ref, count_ref, me_ref, src_ref, turn_refs, turn_sem)
    own.wait()
    wait_all(turn_refs, turn_sem)


def slim_shapes(peers, slots, slim, size, kind):
    return [pltpu.HBM((peers // PLANE * slots, slim, size), kind)] * PLANE


def pack_slim(table, counts, me, probes, peers, slots, rows, size):
    part, kind = probes.shape[0], probes.dtype
    return pl.pallas_call(
        pack_slim_kernel,
        in_specs=[SMEM, SMEM, SMEM, VMEM],
        out_specs=[HBM] * (1 + PLANE),
        scratch_shapes=[pltpu.VMEM((rows + 1, part, size), kind), DMA, DMA],
        out_shape=[pltpu.HBM((rows, part, size), kind)] + slim_shapes(peers, slots, part - WIDE, size, kind),
        compiler_params=grant(62),
        name="pack_slim",
    )(table, counts, me, probes)


def turn_kernel(*refs):
    got, out, (held_ref, in_sem, out_sem) = refs[:PLANE], refs[PLANE + 1:-3], refs[-3:]
    slots = out[0].shape[0] // PLANE
    for k, ref in enumerate(got):
        pltpu.make_async_copy(ref, held_ref.at[k], in_sem.at[k]).start()
    for k, ref in enumerate(got):
        pltpu.make_async_copy(ref, held_ref.at[k], in_sem.at[k]).wait()
        for dz, target in enumerate(out):
            pltpu.make_async_copy(
                held_ref.at[k, pl.ds(dz * slots, slots)], target.at[pl.ds(k * slots, slots)], out_sem
            ).start()
    wait_all(out, out_sem)


def turn(got, after):
    blocks, part, size = got[0].shape
    count = blocks // ZS * PLANE
    return pl.pallas_call(
        turn_kernel,
        in_specs=[HBM] * (PLANE + 1),
        out_specs=[HBM] * ZS,
        scratch_shapes=[pltpu.VMEM((PLANE, blocks, part, size), got[0].dtype), DMA((PLANE,)), DMA],
        out_shape=[pltpu.HBM((count, part, size), got[0].dtype)] * ZS,
        compiler_params=grant(62),
        name="turn",
    )(*[in_hbm(x) for x in got], in_hbm(after))


def block_copy(blocks_ref, held_ref, sem, first, count, step):
    rows = pl.ds(step * STEP, STEP)
    return pltpu.make_async_copy(blocks_ref.at[rows, pl.ds(first, count)], held_ref.at[rows], sem.at[step])


def local_products(lane_ref, pieces, blocks_ref, panel_ref, held_ref, panel_sem, sem, cols_ref, use, done=None):
    rows = pieces[0].shape[0]
    steps = rows // STEP
    me = lane_ref[0]
    copies = []
    for n, piece in enumerate(pieces):
        lane = lax.rem(me + LANES - n % LANES, LANES)
        probes = pl.ds(n // LANES * WIDE, piece.shape[1])
        copies.append(
            pltpu.make_async_copy(piece, panel_ref.at[pl.ds(lane * rows, rows), probes], panel_sem.at[n])
        )
    for copy in copies:
        copy.start()
    for step in range(steps):
        block_copy(blocks_ref, held_ref, sem, 0, LOCAL, step).start()
    for copy in copies:
        copy.wait()

    @pl.loop(0, steps)
    def _(step):
        block_copy(blocks_ref, held_ref, sem, 0, LOCAL, step).wait()
        for t in range(STEP):
            r = step * STEP + t
            total = None
            for j in range(0, LOCAL, 2):
                term = pair_dot(
                    [panel_ref[cols_ref[j + k, r]] for k in range(2)],
                    [held_ref[r, j + k] for k in range(2)],
                )
                total = term if total is None else total + term
            use(r, total)
        if done is not None:
            done(step)


def local_kernel(cols_ref, lane_ref, own_ref, prev_ref, across_ref, next_ref, blocks_ref, sum_ref, total_ref, total_sem, panel_ref, held_ref, panel_sem, sem):
    def use(r, total):
        total_ref[r] = total

    def done(step):
        at = pl.ds(step * STEP, STEP)
        pltpu.make_async_copy(total_ref.at[at], sum_ref.at[at], total_sem).start()

    pieces = (own_ref, prev_ref, across_ref, next_ref)
    local_products(lane_ref, pieces, blocks_ref, panel_ref, held_ref, panel_sem, sem, cols_ref, use, done)
    wait_all([sum_ref], total_sem)


def local_scratch(rows, part, size, kind):
    return [
        pltpu.VMEM((LANES * rows, part, size), kind),
        pltpu.VMEM((rows, LOCAL, size, size), kind),
        DMA((2 * LANES,)),
        DMA((rows // STEP,)),
    ]


def in_hbm(x):
    return pltpu.with_memory_space_constraint(x, pltpu.HBM)


def in_vmem(x):
    return pltpu.with_memory_space_constraint(x, pltpu.VMEM)


def local_part(cols, lane, pieces, blocks):
    rows, part, size = pieces[0].shape
    return pl.pallas_call(
        local_kernel,
        in_specs=[SMEM, SMEM] + [HBM] * 5,
        out_specs=HBM,
        scratch_shapes=[pltpu.VMEM((rows, part, size), jnp.float32), DMA] + local_scratch(rows, part, size, blocks.dtype),
        out_shape=pltpu.HBM((rows, part, size), jnp.float32),
        compiler_params=grant(24),
        name="local",
    )(cols, lane, *[in_hbm(x) for x in pieces], in_hbm(blocks))


def row_copies(blocks_ref, other_ref, far_ref, near_ref, far_sem, near_sem, probes, step):
    at = pl.ds(step * STEP, STEP)
    return (
        block_copy(blocks_ref, far_ref, far_sem, LOCAL, REMOTE, step),
        pltpu.make_async_copy(other_ref.at[at, probes], near_ref.at[at], near_sem.at[step]),
    )


def remote_products(fields, blocks_ref, other_ref, probes, far_ref, near_ref, far_sem, near_sem, use, ready=None):
    rows = near_ref.shape[0]
    steps = rows // STEP
    for step in range(steps):
        for copy in row_copies(blocks_ref, other_ref, far_ref, near_ref, far_sem, near_sem, probes, step):
            copy.start()
    if ready is not None:
        ready()

    @pl.loop(0, steps)
    def _(step):
        for copy in row_copies(blocks_ref, other_ref, far_ref, near_ref, far_sem, near_sem, probes, step):
            copy.wait()
        for t in range(STEP):
            r = step * STEP + t
            left = [
                jnp.concatenate([ref[refs[j, r]] for ref, refs in fields], axis=0) for j in range(REMOTE)
            ]
            use(r, pair_dot(left, [far_ref[r, j] for j in range(REMOTE)]), near_ref[r])


def remote_scratch(rows, part, size, kind, near_kind):
    return [
        pltpu.VMEM((rows, REMOTE, size, size), kind),
        pltpu.VMEM((rows, part, size), near_kind),
        DMA((rows // STEP,)),
        DMA((rows // STEP,)),
    ]


def slim_copies(got_refs, panel_ref, sem):
    count = got_refs[0].shape[0]
    return [
        pltpu.make_async_copy(ref, panel_ref.at[pl.ds(dz * count, count)], sem.at[dz]) for dz, ref in enumerate(got_refs)
    ]


def first_wide_kernel(refs_ref, table_ref, count_ref, got_ref, sum_ref, blocks_ref, own_ref, send_ref, src_ref, own_sem, send_sem, *scratch):
    rows, part, _ = own_ref.shape
    src_ref[rows] = jnp.zeros_like(src_ref[rows])

    def use(r, total, near):
        src_ref[r] = (near + total).astype(src_ref.dtype)

    remote_products([(got_ref, refs_ref)], blocks_ref, sum_ref, pl.ds(0, part), *scratch, use)
    start_wide(table_ref, count_ref, src_ref, send_ref, send_sem)
    own = pltpu.make_async_copy(src_ref.at[pl.ds(0, rows)], own_ref, own_sem)
    own.start()
    own.wait()
    wait_all([send_ref], send_sem)


def first_wide(refs, table, counts, got, sums, blocks, peers, slots):
    rows, _, size = sums.shape
    kind = got.dtype
    return pl.pallas_call(
        first_wide_kernel,
        in_specs=[SMEM, SMEM, SMEM, VMEM, HBM, HBM],
        out_specs=[HBM, HBM],
        scratch_shapes=[pltpu.VMEM((rows + 1, WIDE, size), kind), DMA, DMA]
        + remote_scratch(rows, WIDE, size, kind, sums.dtype),
        out_shape=[pltpu.HBM((rows, WIDE, size), kind), pltpu.HBM((peers, slots, WIDE, size), kind)],
        compiler_params=grant(24),
        name="first_wide",
    )(refs, table, counts, in_vmem(got), in_hbm(sums), in_hbm(blocks))


def first_slim_kernel(refs_ref, table_ref, count_ref, me_ref, *rest):
    got_refs, (sum_ref, blocks_ref, own_ref), rest = rest[:ZS], rest[ZS:ZS + 3], rest[ZS + 3:]
    turn_refs, (src_ref, panel_ref, own_sem, turn_sem, got_sem), scratch = rest[:PLANE], rest[PLANE:PLANE + 5], rest[PLANE + 5:]
    rows, part, _ = own_ref.shape
    src_ref[rows] = jnp.zeros_like(src_ref[rows])
    copies = slim_copies(got_refs, panel_ref, got_sem)
    for copy in copies:
        copy.start()

    def ready():
        for copy in copies:
            copy.wait()

    def use(r, total, near):
        src_ref[r] = (near + total).astype(src_ref.dtype)

    remote_products([(panel_ref, refs_ref)], blocks_ref, sum_ref, pl.ds(WIDE, part), *scratch, use, ready)
    start_slim(0, table_ref, count_ref, me_ref, src_ref, turn_refs, turn_sem)
    own = pltpu.make_async_copy(src_ref.at[pl.ds(0, rows)], own_ref, own_sem)
    own.start()
    own.wait()
    wait_all(turn_refs, turn_sem)


def first_slim(refs, table, counts, me, got, sums, blocks, peers, slots):
    rows, part, size = sums.shape
    slim, kind = part - WIDE, got[0].dtype
    return pl.pallas_call(
        first_slim_kernel,
        in_specs=[SMEM] * 4 + [HBM] * (ZS + 2),
        out_specs=[HBM] * (1 + PLANE),
        scratch_shapes=[
            pltpu.VMEM((rows + 1, slim, size), kind),
            pltpu.VMEM((peers * slots, slim, size), kind),
            DMA,
            DMA,
            DMA((ZS,)),
        ]
        + remote_scratch(rows, slim, size, kind, sums.dtype),
        out_shape=[pltpu.HBM((rows, slim, size), kind)] + slim_shapes(peers, slots, slim, size, kind),
        compiler_params=grant(24),
        name="first_slim",
    )(refs, table, counts, me, *[in_hbm(x) for x in got], in_hbm(sums), in_hbm(blocks))


def near_kernel(scale, cols_ref, lane_ref, *rest):
    pieces, rest = rest[:2 * LANES], rest[2 * LANES:]
    blocks_ref, probes_ref, near_ref, base_ref, panel_ref, held_ref, base_sem, panel_sem, sem = rest
    rows, _, size = base_ref.shape
    copy = pltpu.make_async_copy(probes_ref, base_ref, base_sem)
    copy.start()
    copy.wait()
    me = lane_ref[0]

    def use(r, total):
        base = base_ref[r].astype(jnp.float32)
        one = panel_ref[me * rows + r].astype(jnp.float32)
        at = pl.ds(pl.multiple_of(r * size, size), size)
        for k, other in enumerate((base, one, 2.0 * total - base)):
            value = jnp.sum(base * other, axis=0, keepdims=True)
            near_ref[k:k + 1, at] = value if scale[k] is None else value * scale[k]

    local_products(lane_ref, pieces, blocks_ref, panel_ref, held_ref, panel_sem, sem, cols_ref, use)


def near_part(cols, lane, pieces, blocks, base, scale):
    rows, part, size = base.shape
    panel, held, panel_sem, sem = local_scratch(rows, part, size, blocks.dtype)
    return pl.pallas_call(
        functools.partial(near_kernel, scale),
        in_specs=[SMEM, SMEM] + [HBM] * (2 * LANES + 2),
        out_specs=VMEM,
        scratch_shapes=[pltpu.VMEM(base.shape, base.dtype), panel, held, DMA, panel_sem, sem],
        out_shape=jax.ShapeDtypeStruct((3, rows * size), jnp.float32),
        compiler_params=grant(24),
        name="near",
    )(cols, lane, *[in_hbm(x) for x in pieces], in_hbm(blocks), in_hbm(base))


def moment_row(scale, near_ref, out_ref, size):
    out_ref[0:2] = near_ref[0:2]

    def use(r, total, base):
        at = pl.ds(pl.multiple_of(r * size, size), size)
        value = near_ref[2:3, at] + 2.0 * jnp.sum(total * base.astype(jnp.float32), axis=0, keepdims=True)
        out_ref[2:3, at] = value if scale is None else value * scale

    return use


def wide_kernel(refs_ref, wide_ref, near_ref, base_ref, blocks_ref, out_ref, *scratch):
    use = moment_row(None, near_ref, out_ref, base_ref.shape[2])
    remote_products([(wide_ref, refs_ref)], blocks_ref, base_ref, pl.ds(0, WIDE), *scratch, use)


def wide_part(refs, wide, near, base, blocks):
    rows, _, size = base.shape
    return pl.pallas_call(
        wide_kernel,
        in_specs=[SMEM, VMEM, VMEM, HBM, HBM],
        out_specs=VMEM,
        scratch_shapes=remote_scratch(rows, WIDE, size, blocks.dtype, base.dtype),
        out_shape=jax.ShapeDtypeStruct(near.shape, near.dtype),
        compiler_params=grant(24),
        name="wide",
    )(refs, in_vmem(wide), near, in_hbm(base), in_hbm(blocks))


def moments_kernel(scale, refs_ref, *rest):
    got_refs, (near_ref, base_ref, blocks_ref, out_ref, panel_ref, got_sem), scratch = rest[:ZS], rest[ZS:ZS + 6], rest[ZS + 6:]
    copies = slim_copies(got_refs, panel_ref, got_sem)
    for copy in copies:
        copy.start()
    _, part, size = base_ref.shape

    def ready():
        for copy in copies:
            copy.wait()

    use = moment_row(scale, near_ref, out_ref, size)
    remote_products([(panel_ref, refs_ref)], blocks_ref, base_ref, pl.ds(WIDE, part - WIDE), *scratch, use, ready)


def moments_part(refs, got, near, base, blocks, scale):
    rows, part, size = base.shape
    slim = part - WIDE
    return pl.pallas_call(
        functools.partial(moments_kernel, scale),
        in_specs=[SMEM] + [HBM] * ZS + [VMEM, HBM, HBM],
        out_specs=VMEM,
        scratch_shapes=[pltpu.VMEM((ZS * got[0].shape[0], slim, size), base.dtype), DMA((ZS,))]
        + remote_scratch(rows, slim, size, blocks.dtype, base.dtype),
        out_shape=jax.ShapeDtypeStruct(near.shape, near.dtype),
        compiler_params=grant(24),
        name="moments",
    )(refs, *[in_hbm(x) for x in got], near, in_hbm(base), in_hbm(blocks))


def plane_step(i, k):
    z, x, core = i // PLANE, i // CS % XS, i % CS
    return z * PLANE + (x + k // CS) % XS * CS + (core + k) % CS


def across_plane(sends):
    size = ZS * PLANE
    return [sends[0]] + [
        lax.ppermute(sends[k], "dom", [(i, plane_step(i, k)) for i in range(size)]) for k in range(1, PLANE)
    ]


def along_z(sends, steps):
    size = ZS * PLANE
    return {dz: lax.ppermute(sends[dz], "dom", [(i, (i + dz * PLANE) % size) for i in range(size)]) for dz in steps}


def slim_kernel(me_ref, refs_ref, out_ref, *, slots):
    me = me_ref[0]
    refs = refs_ref[...]
    e = refs // slots
    dz = (me // PLANE - e // PLANE) & (ZS - 1)
    dx = (me // CS - e // CS) & (XS - 1)
    core = (me - e) & (CS - 1)
    out_ref[...] = (dz * PLANE + dx * CS + core) * slots + refs - e * slots


def slim_slots(refs, slots, me):
    return pl.pallas_call(
        functools.partial(slim_kernel, slots=slots),
        in_specs=[SMEM, VMEM],
        out_specs=VMEM,
        out_shape=jax.ShapeDtypeStruct(refs.shape, refs.dtype),
        compiler_params=grant(62),
        name="slim_slots",
    )(me, refs)


def on_device(blocks, local_cols, remote_refs, send_blocks, send_counts, probes):
    rows, _, size, _ = blocks.shape
    peers, slots = send_blocks.shape[2], send_blocks.shape[3]
    table = send_blocks.transpose(0, 3, 1, 2)[0]
    counts = send_counts[0, 0]
    cols = local_cols.T
    refs = remote_refs.T
    lane = lax.axis_index("grp").astype(jnp.int32).reshape(1)
    me = lax.axis_index("dom").astype(jnp.int32).reshape(1)
    norm = 1.0 / math.sqrt(PROBES)
    scale = (
        jackson(0, KMOM) * norm,
        2.0 * jackson(1, KMOM) * norm,
        2.0 * jackson(2, KMOM) * norm,
    )

    def exchange(send):
        got = lax.all_to_all(send, "dom", split_axis=0, concat_axis=0, tiled=True)
        return got.reshape(peers * slots, send.shape[2], size)

    def panel(own):
        pieces = [own]
        for shift in (1, 2, 3):
            pieces.append(lax.ppermute(own, "grp", [(i, (i + shift) % LANES) for i in range(LANES)]))
        return pieces

    send = pack_wide(table, counts, probes, peers, slots, rows, size)
    wide = exchange(send)
    base, *sides = pack_slim(table, counts, me, probes, peers, slots, rows, size)
    sides = across_plane(sides)
    pieces = panel(base)
    sides = turn(sides, base)
    slim = {0: sides[0]} | along_z(sides, EARLY)
    sums = local_part(cols, lane, pieces, blocks)
    slim |= along_z(sides, LATE)
    slim = [slim[dz] for dz in range(ZS)]
    slim_refs = slim_slots(refs, slots, me)
    first, send = first_wide(refs, table, counts, wide, sums, blocks, peers, slots)
    wide = exchange(send)
    pieces = panel(first)
    slim_first, *sides = first_slim(slim_refs, table, counts, me, slim, sums, blocks, peers, slots)
    sides = across_plane(sides)
    pieces = pieces + panel(slim_first)
    sides = turn(sides, slim_first)
    slim = {0: sides[0]} | along_z(sides, (4, 3, 5, 2, 6, 1, 7))
    slim = [slim[dz] for dz in range(ZS)]
    near = near_part(cols, lane, pieces, blocks, base, scale[:2] + (None,))
    near = wide_part(refs, wide, near, base, blocks)
    return moments_part(slim_refs, slim, near, base, blocks, scale[2])


def solution(mesh):
    in_specs = (
        P(("dom", "grp"), None, None, None),
        P(("dom", "grp"), None),
        P(("dom", "grp"), None),
        P("dom", "grp", None, None),
        P("dom", "grp", None),
        P(None, ("dom", "grp")),
    )
    out_specs = P(None, ("dom", "grp"))

    return jax.shard_map(on_device, mesh=mesh, in_specs=in_specs, out_specs=out_specs, check_vma=False)
```

```python
import functools
import math

import jax
import jax.numpy as jnp
from jax import lax
from jax.experimental import pallas as pl
from jax.experimental.pallas import tpu as pltpu
from jax.sharding import PartitionSpec as P


PROBES = 64
LOCAL = 4
REMOTE = 2
KMOM = 256
LANES = 4
STEP = 8
WIDE = 48
ZS, XS, CS = 8, 4, 2
PLANE = XS * CS
EARLY, LATE = (1, 7, 2, 6, 3), (5, 4)


def grant(mib):
    return pltpu.CompilerParams(vmem_limit_bytes=mib * 1024 * 1024)


HBM = pl.BlockSpec(memory_space=pltpu.HBM)
VMEM = pl.BlockSpec(memory_space=pltpu.VMEM)
ANY = pl.BlockSpec(memory_space=pl.ANY)
SMEM = pl.BlockSpec(memory_space=pltpu.SMEM)
DMA = pltpu.SemaphoreType.DMA


def jackson(order, total):
    angle = math.pi / (total + 1)
    return (
        (total - order + 1) * math.cos(order * angle) + math.sin(order * angle) / math.tan(angle)
    ) / (total + 1)


def pair_dot(fields, mats):
    left = jnp.concatenate(fields, axis=1)
    right = jnp.concatenate(mats, axis=1)
    return lax.dot_general(left, right, (((1,), (1,)), ((), ())), preferred_element_type=jnp.float32)


def start_wide(table_ref, count_ref, src_ref, send_ref, sem):
    rows = src_ref.shape[0] - 1
    peers, slots, part, _ = send_ref.shape
    probes = pl.ds(0, part)

    @pl.loop(0, peers, unroll=4)
    def _(d):
        count = count_ref[d]
        for s in range(slots):
            index = jnp.where(s < count, table_ref[s, 0, d], rows)
            pltpu.make_async_copy(src_ref.at[index, probes], send_ref.at[d, s], sem).start()


def start_slim(first, table_ref, count_ref, me_ref, src_ref, turn_refs, sem):
    rows = src_ref.shape[0] - 1
    part = turn_refs[0].shape[1]
    slots = turn_refs[0].shape[0] // ZS
    me = me_ref[0]
    probes = pl.ds(first, part)

    @pl.loop(0, ZS)
    def _(dz):
        z = (me // PLANE + dz) & (ZS - 1)
        for k, ref in enumerate(turn_refs):
            x = (me // CS + k // CS) & (XS - 1)
            core = (me + k) & (CS - 1)
            d = z * PLANE + x * CS + core
            for s in range(slots):
                index = jnp.where(s < count_ref[d], table_ref[s, 0, d], rows)
                pltpu.make_async_copy(src_ref.at[index, probes], ref.at[dz * slots + s], sem).start()


def wait_all(refs, sem):
    for ref in refs:
        pltpu.make_async_copy(ref, ref, sem).wait()


def load_fields(probes_ref, src_ref):
    rows, size = src_ref.shape[0] - 1, src_ref.shape[2]
    for r in range(rows):
        src_ref[r] = probes_ref[:, r * size:(r + 1) * size]
    src_ref[rows] = jnp.zeros_like(src_ref[rows])


def pack_wide_kernel(table_ref, count_ref, probes_ref, send_ref, src_ref, send_sem):
    load_fields(probes_ref, src_ref)
    start_wide(table_ref, count_ref, src_ref, send_ref, send_sem)
    wait_all([send_ref], send_sem)


def pack_wide(table, counts, probes, peers, slots, rows, size):
    kind = probes.dtype
    return pl.pallas_call(
        pack_wide_kernel,
        grid=(1,),
        in_specs=[SMEM, SMEM, pl.BlockSpec((WIDE, probes.shape[1]), lambda i: (0, 0))],
        out_specs=HBM,
        scratch_shapes=[pltpu.VMEM((rows + 1, WIDE, size), kind), DMA],
        out_shape=pltpu.HBM((peers, slots, WIDE, size), kind),
        compiler_params=grant(62),
        name="pack_wide",
    )(table, counts, probes)


def pack_slim_kernel(table_ref, count_ref, me_ref, probes_ref, own_ref, *rest):
    turn_refs, (src_ref, own_sem, turn_sem) = rest[:PLANE], rest[PLANE:]
    rows = own_ref.shape[0]
    load_fields(probes_ref, src_ref)
    own = pltpu.make_async_copy(src_ref.at[pl.ds(0, rows)], own_ref, own_sem)
    own.start()
    start_slim(WIDE, table_ref, count_ref, me_ref, src_ref, turn_refs, turn_sem)
    own.wait()
    wait_all(turn_refs, turn_sem)


def slim_shapes(peers, slots, slim, size, kind):
    return [pltpu.HBM((peers // PLANE * slots, slim, size), kind)] * PLANE


def pack_slim(table, counts, me, probes, peers, slots, rows, size):
    part, kind = probes.shape[0], probes.dtype
    return pl.pallas_call(
        pack_slim_kernel,
        in_specs=[SMEM, SMEM, SMEM, VMEM],
        out_specs=[HBM] * (1 + PLANE),
        scratch_shapes=[pltpu.VMEM((rows + 1, part, size), kind), DMA, DMA],
        out_shape=[pltpu.HBM((rows, part, size), kind)] + slim_shapes(peers, slots, part - WIDE, size, kind),
        compiler_params=grant(24),
        name="pack_slim",
    )(table, counts, me, probes)


def turn_kernel(*refs):
    got, out, (held_ref, in_sem, out_sem) = refs[:PLANE], refs[PLANE + 1:-3], refs[-3:]
    slots = out[0].shape[0] // PLANE
    for k, ref in enumerate(got):
        pltpu.make_async_copy(ref, held_ref.at[k], in_sem.at[k]).start()
    for k, ref in enumerate(got):
        pltpu.make_async_copy(ref, held_ref.at[k], in_sem.at[k]).wait()
        for dz, target in enumerate(out):
            pltpu.make_async_copy(
                held_ref.at[k, pl.ds(dz * slots, slots)], target.at[pl.ds(k * slots, slots)], out_sem
            ).start()
    wait_all(out, out_sem)


def turn(got, after):
    blocks, part, size = got[0].shape
    count = blocks // ZS * PLANE
    return pl.pallas_call(
        turn_kernel,
        in_specs=[ANY] * PLANE + [HBM],
        out_specs=[HBM] * ZS,
        scratch_shapes=[pltpu.VMEM((PLANE, blocks, part, size), got[0].dtype), DMA((PLANE,)), DMA],
        out_shape=[pltpu.HBM((count, part, size), got[0].dtype)] * ZS,
        compiler_params=grant(24),
        name="turn",
    )(*got, in_hbm(after))


def block_copy(blocks_ref, held_ref, sem, first, count, step):
    rows = pl.ds(step * STEP, STEP)
    return pltpu.make_async_copy(blocks_ref.at[rows, pl.ds(first, count)], held_ref.at[rows], sem.at[step])


def fetch_kernel(blocks_ref, close_ref, sem):
    copy = pltpu.make_async_copy(blocks_ref.at[:, pl.ds(0, LOCAL)], close_ref, sem)
    copy.start()
    copy.wait()


def fetch(blocks):
    rows, _, size, _ = blocks.shape
    return pl.pallas_call(
        fetch_kernel,
        in_specs=[HBM],
        out_specs=VMEM,
        scratch_shapes=[DMA],
        out_shape=pltpu.VMEM((rows, LOCAL, size, size), blocks.dtype),
        compiler_params=grant(24),
        name="fetch",
    )(in_hbm(blocks))


def local_products(lane_ref, pieces, blocks_ref, panel_ref, held_ref, panel_sem, sem, cols_ref, use, done=None):
    rows = pieces[0].shape[0]
    steps = rows // STEP
    me = lane_ref[0]
    copies = []
    for n, piece in enumerate(pieces):
        lane = lax.rem(me + LANES - n % LANES, LANES)
        probes = pl.ds(n // LANES * WIDE, piece.shape[1])
        copies.append(
            pltpu.make_async_copy(piece, panel_ref.at[pl.ds(lane * rows, rows), probes], panel_sem.at[n])
        )
    for copy in copies:
        copy.start()
    if blocks_ref is not None:
        for step in range(steps):
            block_copy(blocks_ref, held_ref, sem, 0, LOCAL, step).start()
    for copy in copies:
        copy.wait()

    @pl.loop(0, steps)
    def _(step):
        if blocks_ref is not None:
            block_copy(blocks_ref, held_ref, sem, 0, LOCAL, step).wait()
        for t in range(STEP):
            r = step * STEP + t
            total = None
            for j in range(0, LOCAL, 2):
                term = pair_dot(
                    [panel_ref[cols_ref[j + k, r]] for k in range(2)],
                    [held_ref[r, j + k] for k in range(2)],
                )
                total = term if total is None else total + term
            use(r, total)
        if done is not None:
            done(step)


def local_kernel(cols_ref, lane_ref, own_ref, prev_ref, across_ref, next_ref, close_ref, sum_ref, total_ref, total_sem, panel_ref, panel_sem):
    def use(r, total):
        total_ref[r] = total

    def done(step):
        at = pl.ds(step * STEP, STEP)
        pltpu.make_async_copy(total_ref.at[at], sum_ref.at[at], total_sem).start()

    pieces = (own_ref, prev_ref, across_ref, next_ref)
    local_products(lane_ref, pieces, None, panel_ref, close_ref, panel_sem, None, cols_ref, use, done)
    wait_all([sum_ref], total_sem)


def local_scratch(rows, part, size, kind):
    return [
        pltpu.VMEM((LANES * rows, part, size), kind),
        pltpu.VMEM((rows, LOCAL, size, size), kind),
        DMA((2 * LANES,)),
        DMA((rows // STEP,)),
    ]


def in_hbm(x):
    return pltpu.with_memory_space_constraint(x, pltpu.HBM)


def in_vmem(x):
    return pltpu.with_memory_space_constraint(x, pltpu.VMEM)


def local_part(cols, lane, pieces, close):
    rows, part, size = pieces[0].shape
    panel, _, panel_sem, _ = local_scratch(rows, part, size, close.dtype)
    return pl.pallas_call(
        local_kernel,
        in_specs=[SMEM, SMEM] + [ANY] * LANES + [VMEM],
        out_specs=HBM,
        scratch_shapes=[pltpu.VMEM((rows, part, size), jnp.float32), DMA, panel, panel_sem],
        out_shape=pltpu.HBM((rows, part, size), jnp.float32),
        compiler_params=grant(24),
        name="local",
    )(cols, lane, *pieces, in_vmem(close))


def row_copies(blocks_ref, other_ref, far_ref, near_ref, far_sem, near_sem, probes, step):
    at = pl.ds(step * STEP, STEP)
    near = pltpu.make_async_copy(other_ref.at[at, probes], near_ref.at[at], near_sem.at[step])
    return block_copy(blocks_ref, far_ref, far_sem, LOCAL, REMOTE, step), near


def remote_products(gather, left, blocks_ref, other_ref, probes, far_ref, near_ref, far_sem, near_sem, use):
    rows = near_ref.shape[0]
    steps = rows // STEP
    start, wait = gather
    for step in range(steps):
        start(step)
        for copy in row_copies(blocks_ref, other_ref, far_ref, near_ref, far_sem, near_sem, probes, step):
            copy.start()

    @pl.loop(0, steps)
    def _(step):
        wait(step)
        for copy in row_copies(blocks_ref, other_ref, far_ref, near_ref, far_sem, near_sem, probes, step):
            copy.wait()
        for t in range(STEP):
            r = step * STEP + t
            use(r, pair_dot([left(j, r) for j in range(REMOTE)], [far_ref[r, j] for j in range(REMOTE)]), near_ref[r])


def held_wide(refs_ref, got_ref):
    return (lambda step: None, lambda step: None), lambda j, r: got_ref[refs_ref[j, r]]


def gather_slim(refs_ref, got_refs, panel_ref, sem):
    copies = slim_copies(got_refs, panel_ref, sem)

    def start(step):
        if step == 0:
            for copy in copies:
                copy.start()

    def wait(step):
        @pl.when(step == 0)
        def _():
            for copy in copies:
                copy.wait()

    return (start, wait), lambda j, r: panel_ref[refs_ref[j, r]]


def remote_scratch(rows, part, size, kind, near_kind):
    return [
        pltpu.VMEM((rows, REMOTE, size, size), kind),
        pltpu.VMEM((rows, part, size), near_kind),
        DMA((rows // STEP,)),
        DMA((rows // STEP,)),
    ]


def slim_copies(got_refs, panel_ref, sem):
    count = got_refs[0].shape[0]
    return [
        pltpu.make_async_copy(ref, panel_ref.at[pl.ds(dz * count, count)], sem.at[dz]) for dz, ref in enumerate(got_refs)
    ]


def first_wide_kernel(refs_ref, table_ref, count_ref, got_ref, sum_ref, blocks_ref, own_ref, send_ref, src_ref, own_sem, send_sem, *scratch):
    rows, part, _ = own_ref.shape
    src_ref[rows] = jnp.zeros_like(src_ref[rows])

    def use(r, total, near):
        src_ref[r] = (near + total).astype(src_ref.dtype)

    gather, left = held_wide(refs_ref, got_ref)
    remote_products(gather, left, blocks_ref, sum_ref, pl.ds(0, part), *scratch, use)
    start_wide(table_ref, count_ref, src_ref, send_ref, send_sem)
    own = pltpu.make_async_copy(src_ref.at[pl.ds(0, rows)], own_ref, own_sem)
    own.start()
    own.wait()
    wait_all([send_ref], send_sem)


def first_wide(refs, table, counts, got, sums, blocks, peers, slots):
    rows, _, size = sums.shape
    kind = got.dtype
    return pl.pallas_call(
        first_wide_kernel,
        in_specs=[SMEM, SMEM, SMEM, VMEM, HBM, HBM],
        out_specs=[HBM, HBM],
        scratch_shapes=[pltpu.VMEM((rows + 1, WIDE, size), kind), DMA, DMA]
        + remote_scratch(rows, WIDE, size, kind, sums.dtype),
        out_shape=[pltpu.HBM((rows, WIDE, size), kind), pltpu.HBM((peers, slots, WIDE, size), kind)],
        compiler_params=grant(24),
        name="first_wide",
    )(in_hbm(refs), in_hbm(table), in_hbm(counts), in_vmem(got), in_hbm(sums), in_hbm(blocks))


def first_slim_kernel(refs_ref, table_ref, count_ref, me_ref, *rest):
    got_refs, (sum_ref, blocks_ref, own_ref), rest = rest[:ZS], rest[ZS:ZS + 3], rest[ZS + 3:]
    turn_refs, (src_ref, panel_ref, own_sem, turn_sem, got_sem), scratch = rest[:PLANE], rest[PLANE:PLANE + 5], rest[PLANE + 5:]
    rows, part, _ = own_ref.shape
    src_ref[rows] = jnp.zeros_like(src_ref[rows])

    def use(r, total, near):
        src_ref[r] = (near + total).astype(src_ref.dtype)

    gather, left = gather_slim(refs_ref, got_refs, panel_ref, got_sem)
    remote_products(gather, left, blocks_ref, sum_ref, pl.ds(WIDE, part), *scratch, use)
    start_slim(0, table_ref, count_ref, me_ref, src_ref, turn_refs, turn_sem)
    own = pltpu.make_async_copy(src_ref.at[pl.ds(0, rows)], own_ref, own_sem)
    own.start()
    own.wait()
    wait_all(turn_refs, turn_sem)


def first_slim(refs, table, counts, me, got, sums, blocks, peers, slots):
    rows, part, size = sums.shape
    slim, kind = part - WIDE, got[0].dtype
    return pl.pallas_call(
        first_slim_kernel,
        in_specs=[SMEM] * 4 + [ANY] * ZS + [HBM] * 2,
        out_specs=[HBM] * (1 + PLANE),
        scratch_shapes=[
            pltpu.VMEM((rows + 1, slim, size), kind),
            pltpu.VMEM((peers * slots, slim, size), kind),
            DMA,
            DMA,
            DMA((ZS,)),
        ]
        + remote_scratch(rows, slim, size, kind, sums.dtype),
        out_shape=[pltpu.HBM((rows, slim, size), kind)] + slim_shapes(peers, slots, slim, size, kind),
        compiler_params=grant(24),
        name="first_slim",
    )(refs, table, counts, me, *got, in_hbm(sums), in_hbm(blocks))


def near_kernel(scale, cols_ref, lane_ref, *rest):
    pieces, rest = rest[:2 * LANES], rest[2 * LANES:]
    blocks_ref, probes_ref, near_ref, base_ref, panel_ref, held_ref, base_sem, panel_sem, sem = rest
    rows, _, size = base_ref.shape
    copy = pltpu.make_async_copy(probes_ref, base_ref, base_sem)
    copy.start()
    copy.wait()
    me = lane_ref[0]

    def use(r, total):
        base = base_ref[r].astype(jnp.float32)
        one = panel_ref[me * rows + r].astype(jnp.float32)
        at = pl.ds(pl.multiple_of(r * size, size), size)
        for k, other in enumerate((base, one, 2.0 * total - base)):
            value = jnp.sum(base * other, axis=0, keepdims=True)
            near_ref[k:k + 1, at] = value if scale[k] is None else value * scale[k]

    local_products(lane_ref, pieces, blocks_ref, panel_ref, held_ref, panel_sem, sem, cols_ref, use)


def near_part(cols, lane, pieces, blocks, base, scale):
    rows, part, size = base.shape
    panel, held, panel_sem, sem = local_scratch(rows, part, size, blocks.dtype)
    return pl.pallas_call(
        functools.partial(near_kernel, scale),
        in_specs=[SMEM, SMEM] + [ANY] * (2 * LANES) + [HBM] * 2,
        out_specs=VMEM,
        scratch_shapes=[pltpu.VMEM(base.shape, base.dtype), panel, held, DMA, panel_sem, sem],
        out_shape=jax.ShapeDtypeStruct((3, rows * size), jnp.float32),
        compiler_params=grant(24),
        name="near",
    )(cols, lane, *pieces, in_hbm(blocks), in_hbm(base))


def moment_row(scale, near_ref, out_ref, size):
    out_ref[0:2] = near_ref[0:2]

    def use(r, total, base):
        at = pl.ds(pl.multiple_of(r * size, size), size)
        value = near_ref[2:3, at] + 2.0 * jnp.sum(total * base.astype(jnp.float32), axis=0, keepdims=True)
        out_ref[2:3, at] = value if scale is None else value * scale

    return use


def wide_kernel(refs_ref, wide_ref, near_ref, base_ref, blocks_ref, out_ref, far_ref, rest_ref, rest_sem, *scratch):
    rest = pltpu.make_async_copy(base_ref.at[:, pl.ds(WIDE, rest_ref.shape[1])], rest_ref, rest_sem)
    rest.start()
    use = moment_row(None, near_ref, out_ref, base_ref.shape[2])
    gather, left = held_wide(refs_ref, wide_ref)
    remote_products(gather, left, blocks_ref, base_ref, pl.ds(0, WIDE), far_ref, *scratch, use)
    rest.wait()


def wide_part(refs, wide, near, base, blocks):
    rows, part, size = base.shape
    far, *others = remote_scratch(rows, WIDE, size, blocks.dtype, base.dtype)
    return pl.pallas_call(
        wide_kernel,
        in_specs=[SMEM, VMEM, VMEM, HBM, HBM],
        out_specs=[VMEM] * 3,
        scratch_shapes=[DMA, *others],
        out_shape=[
            pltpu.VMEM(near.shape, near.dtype),
            pltpu.VMEM(far.shape, blocks.dtype),
            pltpu.VMEM((rows, part - WIDE, size), base.dtype),
        ],
        compiler_params=grant(24),
        name="wide",
    )(refs, in_vmem(wide), near, in_hbm(base), in_hbm(blocks))


def moments_kernel(scale, refs_ref, *rest):
    got_refs, (near_ref, far_ref, base_ref, out_ref, panel_ref, got_sem) = rest[:ZS], rest[ZS:]
    copies = slim_copies(got_refs, panel_ref, got_sem)
    for copy in copies:
        copy.start()
    rows, _, size = base_ref.shape
    use = moment_row(scale, near_ref, out_ref, size)
    for copy in copies:
        copy.wait()

    @pl.loop(0, rows // STEP)
    def _(step):
        for t in range(STEP):
            r = step * STEP + t
            left = [panel_ref[refs_ref[j, r]] for j in range(REMOTE)]
            use(r, pair_dot(left, [far_ref[r, j] for j in range(REMOTE)]), base_ref[r])


def moments_part(refs, got, near, far, base, scale):
    _, slim, size = base.shape
    return pl.pallas_call(
        functools.partial(moments_kernel, scale),
        in_specs=[SMEM] + [ANY] * ZS + [VMEM] * 3,
        out_specs=VMEM,
        scratch_shapes=[pltpu.VMEM((ZS * got[0].shape[0], slim, size), base.dtype), DMA((ZS,))],
        out_shape=jax.ShapeDtypeStruct(near.shape, near.dtype),
        compiler_params=grant(24),
        name="moments",
    )(refs, *got, in_vmem(near), in_vmem(far), in_vmem(base))


def plane_step(i, k):
    z, x, core = i // PLANE, i // CS % XS, i % CS
    return z * PLANE + (x + k // CS) % XS * CS + (core + k) % CS


def across_plane(sends):
    size = ZS * PLANE
    return [sends[0]] + [
        lax.ppermute(sends[k], "dom", [(i, plane_step(i, k)) for i in range(size)]) for k in range(1, PLANE)
    ]


def along_z(sends, steps):
    size = ZS * PLANE
    return {dz: lax.ppermute(sends[dz], "dom", [(i, (i + dz * PLANE) % size) for i in range(size)]) for dz in steps}


def slim_kernel(me_ref, refs_ref, out_ref, *, slots):
    me = me_ref[0]
    refs = refs_ref[...]
    e = refs // slots
    dz = (me // PLANE - e // PLANE) & (ZS - 1)
    dx = (me // CS - e // CS) & (XS - 1)
    core = (me - e) & (CS - 1)
    out_ref[...] = (dz * PLANE + dx * CS + core) * slots + refs - e * slots


def slim_slots(refs, slots, me):
    return pl.pallas_call(
        functools.partial(slim_kernel, slots=slots),
        in_specs=[SMEM, VMEM],
        out_specs=VMEM,
        out_shape=jax.ShapeDtypeStruct(refs.shape, refs.dtype),
        compiler_params=grant(24),
        name="slim_slots",
    )(me, refs)


def on_device(blocks, local_cols, remote_refs, send_blocks, send_counts, probes):
    rows, _, size, _ = blocks.shape
    peers, slots = send_blocks.shape[2], send_blocks.shape[3]
    table = send_blocks.transpose(0, 3, 1, 2)[0]
    counts = send_counts[0, 0]
    cols = local_cols.T
    refs = remote_refs.T
    lane = lax.axis_index("grp").astype(jnp.int32).reshape(1)
    me = lax.axis_index("dom").astype(jnp.int32).reshape(1)
    norm = 1.0 / math.sqrt(PROBES)
    scale = (
        jackson(0, KMOM) * norm,
        2.0 * jackson(1, KMOM) * norm,
        2.0 * jackson(2, KMOM) * norm,
    )

    def exchange(send):
        got = lax.all_to_all(send, "dom", split_axis=0, concat_axis=0, tiled=True)
        return got.reshape(peers * slots, send.shape[2], size)

    def panel(own):
        pieces = [own]
        for shift in (1, 2, 3):
            pieces.append(lax.ppermute(own, "grp", [(i, (i + shift) % LANES) for i in range(LANES)]))
        return pieces

    send = pack_wide(table, counts, probes, peers, slots, rows, size)
    wide = exchange(send)
    base, *sides = pack_slim(table, counts, me, probes, peers, slots, rows, size)
    sides = across_plane(sides)
    pieces = panel(base)
    sides = turn(sides, base)
    slim = {0: sides[0]} | along_z(sides, EARLY)
    close = fetch(blocks)
    sums = local_part(cols, lane, pieces, close)
    slim |= along_z(sides, LATE)
    slim = [slim[dz] for dz in range(ZS)]
    slim_refs = slim_slots(refs, slots, me)
    first, send = first_wide(refs, table, counts, wide, sums, blocks, peers, slots)
    wide = exchange(send)
    pieces = panel(first)
    slim_first, *sides = first_slim(slim_refs, table, counts, me, slim, sums, blocks, peers, slots)
    sides = across_plane(sides)
    pieces = pieces + panel(slim_first)
    sides = turn(sides, slim_first)
    slim = {0: sides[0]} | along_z(sides, (4, 3, 5, 2, 6, 1, 7))
    slim = [slim[dz] for dz in range(ZS)]
    near = near_part(cols, lane, pieces, blocks, base, scale[:2] + (None,))
    near, far, rest = wide_part(refs, wide, near, base, blocks)
    return moments_part(slim_refs, slim, near, far, rest, scale[2])


def solution(mesh):
    in_specs = (
        P(("dom", "grp"), None, None, None),
        P(("dom", "grp"), None),
        P(("dom", "grp"), None),
        P("dom", "grp", None, None),
        P("dom", "grp", None),
        P(None, ("dom", "grp")),
    )
    out_specs = P(None, ("dom", "grp"))

    return jax.shard_map(on_device, mesh=mesh, in_specs=in_specs, out_specs=out_specs, check_vma=False)
```

```python
import functools
import math

import jax
import jax.numpy as jnp
from jax import lax
from jax.experimental import pallas as pl
from jax.experimental.pallas import tpu as pltpu
from jax.sharding import PartitionSpec as P


PROBES = 64
LOCAL = 4
REMOTE = 2
KMOM = 256
LANES = 4
STEP = 8
WIDE = 48
ZS, XS, CS = 8, 4, 2
PLANE = XS * CS
EARLY, LATE = (1, 7, 2, 6, 3), (5, 4)


def grant(mib):
    return pltpu.CompilerParams(vmem_limit_bytes=mib * 1024 * 1024)


HBM = pl.BlockSpec(memory_space=pltpu.HBM)
VMEM = pl.BlockSpec(memory_space=pltpu.VMEM)
ANY = pl.BlockSpec(memory_space=pl.ANY)
SMEM = pl.BlockSpec(memory_space=pltpu.SMEM)
DMA = pltpu.SemaphoreType.DMA


def jackson(order, total):
    angle = math.pi / (total + 1)
    return (
        (total - order + 1) * math.cos(order * angle) + math.sin(order * angle) / math.tan(angle)
    ) / (total + 1)


def pair_dot(fields, mats):
    left = jnp.concatenate(fields, axis=1)
    right = jnp.concatenate(mats, axis=1)
    return lax.dot_general(left, right, (((1,), (1,)), ((), ())), preferred_element_type=jnp.float32)


def start_wide(table_ref, count_ref, src_ref, send_ref, sem):
    rows = src_ref.shape[0] - 1
    peers, slots, part, _ = send_ref.shape
    probes = pl.ds(0, part)

    @pl.loop(0, peers, unroll=4)
    def _(d):
        count = count_ref[d]
        for s in range(slots):
            index = jnp.where(s < count, table_ref[s, 0, d], rows)
            pltpu.make_async_copy(src_ref.at[index, probes], send_ref.at[d, s], sem).start()


def start_slim(first, table_ref, count_ref, me_ref, src_ref, turn_refs, sem):
    rows = src_ref.shape[0] - 1
    part = turn_refs[0].shape[1]
    slots = turn_refs[0].shape[0] // ZS
    me = me_ref[0]
    probes = pl.ds(first, part)

    @pl.loop(0, ZS)
    def _(dz):
        z = (me // PLANE + dz) & (ZS - 1)
        for k, ref in enumerate(turn_refs):
            x = (me // CS + k // CS) & (XS - 1)
            core = (me + k) & (CS - 1)
            d = z * PLANE + x * CS + core
            for s in range(slots):
                index = jnp.where(s < count_ref[d], table_ref[s, 0, d], rows)
                pltpu.make_async_copy(src_ref.at[index, probes], ref.at[dz * slots + s], sem).start()


def wait_all(refs, sem):
    for ref in refs:
        pltpu.make_async_copy(ref, ref, sem).wait()


def load_fields(probes_ref, src_ref):
    rows, size = src_ref.shape[0] - 1, src_ref.shape[2]
    for r in range(rows):
        src_ref[r] = probes_ref[:, r * size:(r + 1) * size]
    src_ref[rows] = jnp.zeros_like(src_ref[rows])


def pack_wide_kernel(table_ref, count_ref, probes_ref, send_ref, src_ref, send_sem):
    load_fields(probes_ref, src_ref)
    start_wide(table_ref, count_ref, src_ref, send_ref, send_sem)
    wait_all([send_ref], send_sem)


def pack_wide(table, counts, probes, peers, slots, rows, size):
    kind = probes.dtype
    return pl.pallas_call(
        pack_wide_kernel,
        grid=(1,),
        in_specs=[SMEM, SMEM, pl.BlockSpec((WIDE, probes.shape[1]), lambda i: (0, 0))],
        out_specs=HBM,
        scratch_shapes=[pltpu.VMEM((rows + 1, WIDE, size), kind), DMA],
        out_shape=pltpu.HBM((peers, slots, WIDE, size), kind),
        compiler_params=grant(62),
        name="pack_wide",
    )(table, counts, probes)


def pack_slim_kernel(table_ref, count_ref, me_ref, probes_ref, own_ref, *rest):
    turn_refs, (src_ref, own_sem, turn_sem) = rest[:PLANE], rest[PLANE:]
    rows = own_ref.shape[0]
    load_fields(probes_ref, src_ref)
    own = pltpu.make_async_copy(src_ref.at[pl.ds(0, rows)], own_ref, own_sem)
    own.start()
    start_slim(WIDE, table_ref, count_ref, me_ref, src_ref, turn_refs, turn_sem)
    own.wait()
    wait_all(turn_refs, turn_sem)


def slim_shapes(peers, slots, slim, size, kind):
    return [pltpu.HBM((peers // PLANE * slots, slim, size), kind)] * PLANE


def pack_slim(table, counts, me, probes, peers, slots, rows, size):
    part, kind = probes.shape[0], probes.dtype
    return pl.pallas_call(
        pack_slim_kernel,
        in_specs=[SMEM, SMEM, SMEM, VMEM],
        out_specs=[HBM] * (1 + PLANE),
        scratch_shapes=[pltpu.VMEM((rows + 1, part, size), kind), DMA, DMA],
        out_shape=[pltpu.HBM((rows, part, size), kind)] + slim_shapes(peers, slots, part - WIDE, size, kind),
        compiler_params=grant(24),
        name="pack_slim",
    )(table, counts, me, probes)


def turn_kernel(*refs):
    got, out, (held_ref, in_sem, out_sem) = refs[:PLANE], refs[PLANE + 1:-3], refs[-3:]
    slots = out[0].shape[0] // PLANE
    for k, ref in enumerate(got):
        pltpu.make_async_copy(ref, held_ref.at[k], in_sem.at[k]).start()
    for k, ref in enumerate(got):
        pltpu.make_async_copy(ref, held_ref.at[k], in_sem.at[k]).wait()
        for dz, target in enumerate(out):
            pltpu.make_async_copy(
                held_ref.at[k, pl.ds(dz * slots, slots)], target.at[pl.ds(k * slots, slots)], out_sem
            ).start()
    wait_all(out, out_sem)


def turn(got, after):
    blocks, part, size = got[0].shape
    count = blocks // ZS * PLANE
    return pl.pallas_call(
        turn_kernel,
        in_specs=[ANY] * PLANE + [HBM],
        out_specs=[HBM] * ZS,
        scratch_shapes=[pltpu.VMEM((PLANE, blocks, part, size), got[0].dtype), DMA((PLANE,)), DMA],
        out_shape=[pltpu.HBM((count, part, size), got[0].dtype)] * ZS,
        compiler_params=grant(24),
        name="turn",
    )(*got, in_hbm(after))


def block_copy(blocks_ref, held_ref, sem, first, count, step):
    rows = pl.ds(step * STEP, STEP)
    return pltpu.make_async_copy(blocks_ref.at[rows, pl.ds(first, count)], held_ref.at[rows], sem.at[step])


def fetch_kernel(blocks_ref, close_ref, sem):
    copy = pltpu.make_async_copy(blocks_ref.at[:, pl.ds(0, LOCAL)], close_ref, sem)
    copy.start()
    copy.wait()


def fetch(blocks):
    rows, _, size, _ = blocks.shape
    return pl.pallas_call(
        fetch_kernel,
        in_specs=[HBM],
        out_specs=VMEM,
        scratch_shapes=[DMA],
        out_shape=pltpu.VMEM((rows, LOCAL, size, size), blocks.dtype),
        compiler_params=grant(24),
        name="fetch",
    )(in_hbm(blocks))


def local_products(lane_ref, pieces, blocks_ref, panel_ref, held_ref, panel_sem, sem, cols_ref, use, done=None):
    rows = pieces[0].shape[0]
    steps = rows // STEP
    me = lane_ref[0]
    copies = []
    for n, piece in enumerate(pieces):
        lane = lax.rem(me + LANES - n % LANES, LANES)
        probes = pl.ds(n // LANES * WIDE, piece.shape[1])
        copies.append(
            pltpu.make_async_copy(piece, panel_ref.at[pl.ds(lane * rows, rows), probes], panel_sem.at[n])
        )
    for copy in copies:
        copy.start()
    if blocks_ref is not None:
        for step in range(steps):
            block_copy(blocks_ref, held_ref, sem, 0, LOCAL, step).start()
    for copy in copies:
        copy.wait()

    @pl.loop(0, steps)
    def _(step):
        if blocks_ref is not None:
            block_copy(blocks_ref, held_ref, sem, 0, LOCAL, step).wait()
        for t in range(STEP):
            r = step * STEP + t
            total = None
            for j in range(0, LOCAL, 2):
                term = pair_dot(
                    [panel_ref[cols_ref[j + k, r]] for k in range(2)],
                    [held_ref[r, j + k] for k in range(2)],
                )
                total = term if total is None else total + term
            use(r, total)
        if done is not None:
            done(step)


def local_kernel(cols_ref, lane_ref, own_ref, prev_ref, across_ref, next_ref, close_ref, sum_ref, total_ref, total_sem, panel_ref, panel_sem):
    def use(r, total):
        total_ref[r] = total

    def done(step):
        at = pl.ds(step * STEP, STEP)
        pltpu.make_async_copy(total_ref.at[at], sum_ref.at[at], total_sem).start()

    pieces = (own_ref, prev_ref, across_ref, next_ref)
    local_products(lane_ref, pieces, None, panel_ref, close_ref, panel_sem, None, cols_ref, use, done)
    wait_all([sum_ref], total_sem)


def local_scratch(rows, part, size, kind):
    return [
        pltpu.VMEM((LANES * rows, part, size), kind),
        pltpu.VMEM((rows, LOCAL, size, size), kind),
        DMA((2 * LANES,)),
        DMA((rows // STEP,)),
    ]


def in_hbm(x):
    return pltpu.with_memory_space_constraint(x, pltpu.HBM)


def in_vmem(x):
    return pltpu.with_memory_space_constraint(x, pltpu.VMEM)


def local_part(cols, lane, pieces, close):
    rows, part, size = pieces[0].shape
    panel, _, panel_sem, _ = local_scratch(rows, part, size, close.dtype)
    return pl.pallas_call(
        local_kernel,
        in_specs=[SMEM, SMEM] + [ANY] * LANES + [VMEM],
        out_specs=HBM,
        scratch_shapes=[pltpu.VMEM((rows, part, size), jnp.float32), DMA, panel, panel_sem],
        out_shape=pltpu.HBM((rows, part, size), jnp.float32),
        compiler_params=grant(24),
        name="local",
    )(cols, lane, *pieces, in_vmem(close))


def row_copies(blocks_ref, other_ref, far_ref, near_ref, far_sem, near_sem, probes, step):
    at = pl.ds(step * STEP, STEP)
    near = pltpu.make_async_copy(other_ref.at[at, probes], near_ref.at[at], near_sem.at[step])
    return block_copy(blocks_ref, far_ref, far_sem, LOCAL, REMOTE, step), near


def remote_products(gather, left, blocks_ref, other_ref, probes, far_ref, near_ref, far_sem, near_sem, use):
    rows = near_ref.shape[0]
    steps = rows // STEP
    start, wait = gather
    for step in range(steps):
        start(step)
        for copy in row_copies(blocks_ref, other_ref, far_ref, near_ref, far_sem, near_sem, probes, step):
            copy.start()

    @pl.loop(0, steps)
    def _(step):
        wait(step)
        for copy in row_copies(blocks_ref, other_ref, far_ref, near_ref, far_sem, near_sem, probes, step):
            copy.wait()
        for t in range(STEP):
            r = step * STEP + t
            use(r, pair_dot([left(j, r) for j in range(REMOTE)], [far_ref[r, j] for j in range(REMOTE)]), near_ref[r])


def held_wide(refs_ref, got_ref):
    return (lambda step: None, lambda step: None), lambda j, r: got_ref[refs_ref[j, r]]


def gather_slim(refs_ref, got_refs, panel_ref, sem):
    copies = slim_copies(got_refs, panel_ref, sem)

    def start(step):
        if step == 0:
            for copy in copies:
                copy.start()

    def wait(step):
        @pl.when(step == 0)
        def _():
            for copy in copies:
                copy.wait()

    return (start, wait), lambda j, r: panel_ref[refs_ref[j, r]]


def remote_scratch(rows, part, size, kind, near_kind):
    return [
        pltpu.VMEM((rows, REMOTE, size, size), kind),
        pltpu.VMEM((rows, part, size), near_kind),
        DMA((rows // STEP,)),
        DMA((rows // STEP,)),
    ]


def slim_copies(got_refs, panel_ref, sem):
    count = got_refs[0].shape[0]
    return [
        pltpu.make_async_copy(ref, panel_ref.at[pl.ds(dz * count, count)], sem.at[dz]) for dz, ref in enumerate(got_refs)
    ]


def first_wide_kernel(refs_ref, table_ref, count_ref, got_ref, sum_ref, blocks_ref, own_ref, send_ref, src_ref, own_sem, send_sem, *scratch):
    rows, part, _ = own_ref.shape
    src_ref[rows] = jnp.zeros_like(src_ref[rows])

    def use(r, total, near):
        src_ref[r] = (near + total).astype(src_ref.dtype)

    gather, left = held_wide(refs_ref, got_ref)
    remote_products(gather, left, blocks_ref, sum_ref, pl.ds(0, part), *scratch, use)
    start_wide(table_ref, count_ref, src_ref, send_ref, send_sem)
    own = pltpu.make_async_copy(src_ref.at[pl.ds(0, rows)], own_ref, own_sem)
    own.start()
    own.wait()
    wait_all([send_ref], send_sem)


def first_wide(refs, table, counts, got, sums, blocks, peers, slots):
    rows, _, size = sums.shape
    kind = got.dtype
    return pl.pallas_call(
        first_wide_kernel,
        in_specs=[SMEM, SMEM, SMEM, VMEM, HBM, HBM],
        out_specs=[HBM, HBM],
        scratch_shapes=[pltpu.VMEM((rows + 1, WIDE, size), kind), DMA, DMA]
        + remote_scratch(rows, WIDE, size, kind, sums.dtype),
        out_shape=[pltpu.HBM((rows, WIDE, size), kind), pltpu.HBM((peers, slots, WIDE, size), kind)],
        compiler_params=grant(24),
        name="first_wide",
    )(in_hbm(refs), in_hbm(table), in_hbm(counts), in_vmem(got), in_hbm(sums), in_hbm(blocks))


def first_slim_kernel(refs_ref, table_ref, count_ref, me_ref, *rest):
    got_refs, (sum_ref, blocks_ref, own_ref), rest = rest[:ZS], rest[ZS:ZS + 3], rest[ZS + 3:]
    turn_refs, (src_ref, panel_ref, own_sem, turn_sem, got_sem), scratch = rest[:PLANE], rest[PLANE:PLANE + 5], rest[PLANE + 5:]
    rows, part, _ = own_ref.shape
    src_ref[rows] = jnp.zeros_like(src_ref[rows])

    def use(r, total, near):
        src_ref[r] = (near + total).astype(src_ref.dtype)

    gather, left = gather_slim(refs_ref, got_refs, panel_ref, got_sem)
    remote_products(gather, left, blocks_ref, sum_ref, pl.ds(WIDE, part), *scratch, use)
    start_slim(0, table_ref, count_ref, me_ref, src_ref, turn_refs, turn_sem)
    own = pltpu.make_async_copy(src_ref.at[pl.ds(0, rows)], own_ref, own_sem)
    own.start()
    own.wait()
    wait_all(turn_refs, turn_sem)


def first_slim(refs, table, counts, me, got, sums, blocks, peers, slots):
    rows, part, size = sums.shape
    slim, kind = part - WIDE, got[0].dtype
    return pl.pallas_call(
        first_slim_kernel,
        in_specs=[SMEM] * 4 + [ANY] * ZS + [HBM] * 2,
        out_specs=[HBM] * (1 + PLANE),
        scratch_shapes=[
            pltpu.VMEM((rows + 1, slim, size), kind),
            pltpu.VMEM((peers * slots, slim, size), kind),
            DMA,
            DMA,
            DMA((ZS,)),
        ]
        + remote_scratch(rows, slim, size, kind, sums.dtype),
        out_shape=[pltpu.HBM((rows, slim, size), kind)] + slim_shapes(peers, slots, slim, size, kind),
        compiler_params=grant(24),
        name="first_slim",
    )(in_hbm(refs), in_hbm(table), in_hbm(counts), me, *got, in_hbm(sums), in_hbm(blocks))


def near_kernel(scale, cols_ref, lane_ref, *rest):
    pieces, rest = rest[:2 * LANES], rest[2 * LANES:]
    blocks_ref, probes_ref, near_ref, base_ref, panel_ref, held_ref, base_sem, panel_sem, sem = rest
    rows, _, size = base_ref.shape
    copy = pltpu.make_async_copy(probes_ref, base_ref, base_sem)
    copy.start()
    copy.wait()
    me = lane_ref[0]

    def use(r, total):
        base = base_ref[r].astype(jnp.float32)
        one = panel_ref[me * rows + r].astype(jnp.float32)
        at = pl.ds(pl.multiple_of(r * size, size), size)
        for k, other in enumerate((base, one, 2.0 * total - base)):
            value = jnp.sum(base * other, axis=0, keepdims=True)
            near_ref[k:k + 1, at] = value if scale[k] is None else value * scale[k]

    local_products(lane_ref, pieces, blocks_ref, panel_ref, held_ref, panel_sem, sem, cols_ref, use)


def near_part(cols, lane, pieces, blocks, base, scale):
    rows, part, size = base.shape
    panel, held, panel_sem, sem = local_scratch(rows, part, size, blocks.dtype)
    return pl.pallas_call(
        functools.partial(near_kernel, scale),
        in_specs=[SMEM, SMEM] + [ANY] * (2 * LANES) + [HBM] * 2,
        out_specs=VMEM,
        scratch_shapes=[pltpu.VMEM(base.shape, base.dtype), panel, held, DMA, panel_sem, sem],
        out_shape=jax.ShapeDtypeStruct((3, rows * size), jnp.float32),
        compiler_params=grant(24),
        name="near",
    )(cols, lane, *pieces, in_hbm(blocks), in_hbm(base))


def moment_row(scale, near_ref, out_ref, size):
    out_ref[0:2] = near_ref[0:2]

    def use(r, total, base):
        at = pl.ds(pl.multiple_of(r * size, size), size)
        value = near_ref[2:3, at] + 2.0 * jnp.sum(total * base.astype(jnp.float32), axis=0, keepdims=True)
        out_ref[2:3, at] = value if scale is None else value * scale

    return use


def wide_kernel(refs_ref, wide_ref, near_ref, base_ref, blocks_ref, out_ref, far_ref, rest_ref, rest_sem, *scratch):
    rest = pltpu.make_async_copy(base_ref.at[:, pl.ds(WIDE, rest_ref.shape[1])], rest_ref, rest_sem)
    rest.start()
    use = moment_row(None, near_ref, out_ref, base_ref.shape[2])
    gather, left = held_wide(refs_ref, wide_ref)
    remote_products(gather, left, blocks_ref, base_ref, pl.ds(0, WIDE), far_ref, *scratch, use)
    rest.wait()


def wide_part(refs, wide, near, base, blocks):
    rows, part, size = base.shape
    far, *others = remote_scratch(rows, WIDE, size, blocks.dtype, base.dtype)
    return pl.pallas_call(
        wide_kernel,
        in_specs=[SMEM, VMEM, VMEM, HBM, HBM],
        out_specs=[VMEM] * 3,
        scratch_shapes=[DMA, *others],
        out_shape=[
            pltpu.VMEM(near.shape, near.dtype),
            pltpu.VMEM(far.shape, blocks.dtype),
            pltpu.VMEM((rows, part - WIDE, size), base.dtype),
        ],
        compiler_params=grant(24),
        name="wide",
    )(refs, in_vmem(wide), near, in_hbm(base), in_hbm(blocks))


def moments_kernel(scale, refs_ref, *rest):
    got_refs, (near_ref, far_ref, base_ref, out_ref, panel_ref, got_sem) = rest[:ZS], rest[ZS:]
    copies = slim_copies(got_refs, panel_ref, got_sem)
    for copy in copies:
        copy.start()
    rows, _, size = base_ref.shape
    use = moment_row(scale, near_ref, out_ref, size)
    for copy in copies:
        copy.wait()

    @pl.loop(0, rows // STEP)
    def _(step):
        for t in range(STEP):
            r = step * STEP + t
            left = [panel_ref[refs_ref[j, r]] for j in range(REMOTE)]
            use(r, pair_dot(left, [far_ref[r, j] for j in range(REMOTE)]), base_ref[r])


def moments_part(refs, got, near, far, base, scale):
    _, slim, size = base.shape
    return pl.pallas_call(
        functools.partial(moments_kernel, scale),
        in_specs=[SMEM] + [ANY] * ZS + [VMEM] * 3,
        out_specs=VMEM,
        scratch_shapes=[pltpu.VMEM((ZS * got[0].shape[0], slim, size), base.dtype), DMA((ZS,))],
        out_shape=jax.ShapeDtypeStruct(near.shape, near.dtype),
        compiler_params=grant(24),
        name="moments",
    )(in_hbm(refs), *got, in_vmem(near), in_vmem(far), in_vmem(base))


def plane_step(i, k):
    z, x, core = i // PLANE, i // CS % XS, i % CS
    return z * PLANE + (x + k // CS) % XS * CS + (core + k) % CS


def across_plane(sends):
    size = ZS * PLANE
    return [sends[0]] + [
        lax.ppermute(sends[k], "dom", [(i, plane_step(i, k)) for i in range(size)]) for k in range(1, PLANE)
    ]


def along_z(sends, steps):
    size = ZS * PLANE
    return {dz: lax.ppermute(sends[dz], "dom", [(i, (i + dz * PLANE) % size) for i in range(size)]) for dz in steps}


def slim_kernel(me_ref, refs_ref, out_ref, *, slots):
    me = me_ref[0]
    refs = refs_ref[...]
    e = refs // slots
    dz = (me // PLANE - e // PLANE) & (ZS - 1)
    dx = (me // CS - e // CS) & (XS - 1)
    core = (me - e) & (CS - 1)
    out_ref[...] = (dz * PLANE + dx * CS + core) * slots + refs - e * slots


def slim_slots(refs, slots, me):
    return pl.pallas_call(
        functools.partial(slim_kernel, slots=slots),
        in_specs=[SMEM, VMEM],
        out_specs=VMEM,
        out_shape=jax.ShapeDtypeStruct(refs.shape, refs.dtype),
        compiler_params=grant(24),
        name="slim_slots",
    )(me, refs)


def on_device(blocks, local_cols, remote_refs, send_blocks, send_counts, probes):
    rows, _, size, _ = blocks.shape
    peers, slots = send_blocks.shape[2], send_blocks.shape[3]
    table = send_blocks.transpose(0, 3, 1, 2)[0]
    counts = send_counts[0, 0]
    cols = local_cols.T
    refs = remote_refs.T
    lane = lax.axis_index("grp").astype(jnp.int32).reshape(1)
    me = lax.axis_index("dom").astype(jnp.int32).reshape(1)
    norm = 1.0 / math.sqrt(PROBES)
    scale = (
        jackson(0, KMOM) * norm,
        2.0 * jackson(1, KMOM) * norm,
        2.0 * jackson(2, KMOM) * norm,
    )

    def exchange(send):
        got = lax.all_to_all(send, "dom", split_axis=0, concat_axis=0, tiled=True)
        return got.reshape(peers * slots, send.shape[2], size)

    def panel(own):
        pieces = [own]
        for shift in (1, 2, 3):
            pieces.append(lax.ppermute(own, "grp", [(i, (i + shift) % LANES) for i in range(LANES)]))
        return pieces

    send = pack_wide(table, counts, probes, peers, slots, rows, size)
    wide = exchange(send)
    base, *sides = pack_slim(table, counts, me, probes, peers, slots, rows, size)
    sides = across_plane(sides)
    pieces = panel(base)
    sides = turn(sides, base)
    slim = {0: sides[0]} | along_z(sides, EARLY)
    close = fetch(blocks)
    sums = local_part(cols, lane, pieces, close)
    slim |= along_z(sides, LATE)
    slim = [slim[dz] for dz in range(ZS)]
    slim_refs = slim_slots(refs, slots, me)
    first, send = first_wide(refs, table, counts, wide, sums, blocks, peers, slots)
    wide = exchange(send)
    pieces = panel(first)
    slim_first, *sides = first_slim(slim_refs, table, counts, me, slim, sums, blocks, peers, slots)
    sides = across_plane(sides)
    pieces = pieces + panel(slim_first)
    sides = turn(sides, slim_first)
    slim = {0: sides[0]} | along_z(sides, (4, 3, 5, 2, 6, 7, 1))
    slim = [slim[dz] for dz in range(ZS)]
    near = near_part(cols, lane, pieces, blocks, base, scale[:2] + (None,))
    near, far, rest = wide_part(refs, wide, near, base, blocks)
    return moments_part(slim_refs, slim, near, far, rest, scale[2])


def solution(mesh):
    in_specs = (
        P(("dom", "grp"), None, None, None),
        P(("dom", "grp"), None),
        P(("dom", "grp"), None),
        P("dom", "grp", None, None),
        P("dom", "grp", None),
        P(None, ("dom", "grp")),
    )
    out_specs = P(None, ("dom", "grp"))

    return jax.shard_map(on_device, mesh=mesh, in_specs=in_specs, out_specs=out_specs, check_vma=False)
```
